32 devices in a mesh: expert: 8 (over z, x), hidden: 2 (over core), dp: 2 (over y).
Axes of the slice: x: 2, y: 2, z: 4, core: 2. Of those that a mesh axis runs over, the one named last changes fastest.
Arguments:
- inputs: bfloat16 [384, 4096], P(('expert', 'dp')), may hold values from -6 to 6
- out_grad: bfloat16 [384, 4096], P(('expert', 'dp')), may hold values from -6 to 6
- expert_ids: int32 [384, 6], P(('expert', 'dp')), may hold values from 0 to 15, all different within a row; in each aligned block of 24 rows (0 to 23, 24 to 47, ...) at most 10 rows name the same one
- gate_weights: bfloat16 [384, 6], P(('expert', 'dp')), may hold values from 0.049804688 to 0.59765625
- encode_weight: bfloat16 [4096, 1024], P(None, 'hidden'), may hold values from -0.09375 to 0.09375
- decode_weight: bfloat16 [1024, 4096], P('hidden'), may hold values from -0.1875 to 0.1875
- up_proj: bfloat16 [16, 1024, 2688], P('expert', None, 'hidden'), may hold values from -0.1875 to 0.1875
- down_proj: bfloat16 [16, 2688, 1024], P('expert', 'hidden'), may hold values from -0.125 to 0.125
Outputs:
- latent_grad: float32 [384, 1024], P(('expert', 'dp'), 'hidden')
- gate_dots: bfloat16 [384, 6], P(('expert', 'dp'))
- weight_grad: float32 [16, 2688, 1024], P('expert', 'hidden', 'dp')
The draws below stay inside these ranges and needn't reach their ends.
Inputs may be any that keep to these rules, and one draw needn't show every extreme that they name: `expert_ids`: each row names 6 different experts; within the rows of one token group no expert is named more than 10 times, and the per-expert counts and slot offsets follow from these ids.
All inputs are finite; a program needn't handle non-finite values.
Results may differ from the reference program's by a relative error of at most 0.017.
Values may be sent and summed in bfloat16 or wider, within the bound.
A program may use at most 64 MiB of HBM per device.

```python
import math
import jax
import jax.numpy as jnp
import numpy as np
from jax import lax

D = 4096
LATENT = 1024
HIDDEN_SIZE = 2688
TOP = 6
TOK_DEV = 24
EXPERTS = 16
TOKENS = 384
CAP = 10
N_EXPERT = 8
N_HIDDEN = 2
N_DP = 2


def levels(key, dims, split, least, largest):
    level, own = 1.0, jax.random.fold_in(key, 6)
    for dim, shards_of in split:
        heights = jnp.exp(jax.random.uniform(jax.random.fold_in(own, dim), (shards_of,), jnp.float32, least / len(split), largest / len(split)))
        level = level * jnp.repeat(heights, dims[dim] // shards_of).reshape([-1 if axis == dim else 1 for axis in range(len(dims))])
    return level


def shared_out(stream_key, own, number, rows, count, top, bound, lean):
    sequence = jax.random.permutation(stream_key, count)
    packed, ordinary = load_shares(count, rows * top, bound, lean, True), load_shares(count, rows * top, bound, lean, False)
    places = jnp.arange(count)

    def named(tallies, rotation):
        used = int((tallies > 0).sum())
        fixed = max(1, used // 4)
        shifted = fixed + (places - fixed + rotation * (used - fixed)) % max(1, count - fixed)
        return jnp.zeros((count,), jnp.int32).at[sequence[jnp.where(places < fixed, places, shifted)]].set(jnp.asarray(tallies, jnp.int32))

    tallies = jnp.where(number % 4 == 0, named(packed, number // 4), named(ordinary, number - number // 4 - 1))
    mixed = jax.random.permutation(jax.random.fold_in(own, 3), count)
    giver, taker = mixed[0:count // 2 * 2:2], mixed[1:count // 2 * 2:2]
    room = jnp.minimum(tallies[giver] - 1, bound - tallies[taker]) // 2
    room = jnp.where((giver == sequence[0]) | (taker == sequence[0]) | (tallies[taker] == 0), 0, jnp.maximum(room, 0))
    shifted = jax.random.randint(jax.random.fold_in(own, 4), (count // 2,), 0, 1 << 20) % (room + 1)
    tallies = tallies.at[giver].add(-shifted).at[taker].add(shifted)
    members = jnp.searchsorted(jnp.cumsum(tallies), jnp.arange(rows * top), side="right").astype(jnp.int32)
    listing = members.reshape(top, rows).T
    listing = listing[jax.random.permutation(jax.random.fold_in(own, 1), rows)]
    rotation = jax.random.randint(jax.random.fold_in(own, 2), (rows, 1), 0, top)
    return jnp.take_along_axis(listing, (jnp.arange(top)[None, :] + rotation) % top, axis=1)


def load_shares(count, total, reach, slope, full):
    weights = [(1 << 20) // math.isqrt(grade ** slope) + 1 for grade in range(1, count + 1)]
    largest = reach if full else min(reach, max(-(-total // count), total * weights[0] // sum(weights)))
    least = 1 if total - largest >= count - 1 else 0
    counts, spare = [largest] + [least] * (count - 1), total - largest - least * (count - 1)
    while spare > 0:
        free = [i for i in range(1, count) if counts[i] < largest] or [i for i in range(1, count) if counts[i] < reach]
        whole, remaining = sum([weights[i] for i in free]), spare
        for i in free:
            addition = min(reach - counts[i], max(1, remaining * weights[i] // whole), spare)
            counts[i] = counts[i] + addition
            spare = spare - addition
    return np.array(counts)


def centred(key, dims, spread, most, shards=(), kind=jnp.bfloat16):
    level = levels(key, dims, shards, -0.22, 0.18) if shards else 1.0
    result = jax.random.normal(key, dims, jnp.float32) * spread * level
    return jnp.minimum(jnp.maximum(result, -most), most).astype(kind)


def setup_inputs(seed: int = 0) -> dict:
    key_of = jax.random.split(jax.random.key(seed), 9)
    inputs = centred(key_of[0], (TOKENS, D), 1.0, 6.0, ((0, 16),))
    out_grad = centred(key_of[1], (TOKENS, D), 1.0, 6.0, ((0, 16),))
    expert_ids_keys = jax.random.split(jax.random.fold_in(key_of[2], 1), TOKENS // TOK_DEV)
    expert_ids_turns = jax.random.permutation(jax.random.fold_in(key_of[2], 3), TOKENS // TOK_DEV)
    expert_ids = jax.vmap(lambda own, number: shared_out(jax.random.fold_in(key_of[2], 2), own, number, TOK_DEV, EXPERTS, TOP, CAP, 2))(expert_ids_keys, expert_ids_turns).reshape((TOKENS, TOP))
    gate_weights = jnp.clip(jnp.exp(math.log(0.59765625) - 2.4849066 * jax.random.uniform(key_of[3], (TOKENS, TOP), jnp.float32) ** levels(key_of[3], (TOKENS, TOP), ((0, 16),), -0.2, 0.2)), 0.049804688, 0.59765625).astype(jnp.bfloat16)
    encode_weight = centred(key_of[4], (D, LATENT), D ** -0.5, 0.09375, ((1, 2),))
    decode_weight = centred(key_of[5], (LATENT, D), LATENT ** -0.5, 0.1875, ((0, 2),))
    up_proj = centred(key_of[6], (EXPERTS, LATENT, HIDDEN_SIZE), LATENT ** -0.5, 0.1875, ((0, 8), (2, 2)))
    down_proj = centred(key_of[7], (EXPERTS, HIDDEN_SIZE, LATENT), HIDDEN_SIZE ** -0.5, 0.125, ((0, 8), (1, 2)))
    return dict(inputs=inputs, out_grad=out_grad, expert_ids=expert_ids, gate_weights=gate_weights, encode_weight=encode_weight, decode_weight=decode_weight, up_proj=up_proj, down_proj=down_proj)


def rounded(value):
    return lax.optimization_barrier(value.astype(jnp.bfloat16)).astype(jnp.float32)


def reference(inputs, out_grad, expert_ids, gate_weights, encode_weight, decode_weight, up_proj, down_proj):
    latent_in = jnp.dot(inputs, encode_weight, preferred_element_type=jnp.float32).astype(jnp.bfloat16)
    latent_out = jnp.dot(out_grad, decode_weight.T, preferred_element_type=jnp.float32).astype(jnp.bfloat16)
    groups = TOKENS // TOK_DEV
    ids = expert_ids.reshape(groups, TOK_DEV * TOP)
    onehot = (ids[:, :, None] == jnp.arange(EXPERTS, dtype=jnp.int32)[None, None, :]).astype(jnp.int32)
    slot = jnp.sum((jnp.cumsum(onehot, axis=1) - onehot) * onehot, axis=2)
    group_of = jnp.arange(groups, dtype=jnp.int32)[:, None]
    target = (ids * groups + group_of) * CAP + slot
    pick_ids = jnp.arange(TOKENS * TOP, dtype=jnp.int32).reshape(groups, TOK_DEV * TOP)
    table = jnp.full((EXPERTS * groups * CAP,), -1, jnp.int32)
    table = table.at[target.reshape(-1)].set(pick_ids.reshape(-1)).reshape(EXPERTS, groups * CAP)
    gate_flat = gate_weights.reshape(-1).astype(jnp.float32)
    part_units = HIDDEN_SIZE // N_HIDDEN
    slots = groups * CAP

    def per_expert(carry, inputs_here):
        grad_total, gate_total = carry
        row_table, w_up, w_down = inputs_here
        filled = row_table >= 0
        pick = jnp.maximum(row_table, 0)
        token = pick // TOP
        encoded = jnp.where(filled[:, None], latent_in[token].astype(jnp.float32), 0.0)
        upstream = jnp.where(filled[:, None], latent_out[token].astype(jnp.float32), 0.0)
        weight = jnp.where(filled, gate_flat[pick], 0.0)[:, None]
        up_f = w_up.astype(jnp.float32)
        pre = jnp.dot(encoded, up_f)
        active = jnp.maximum(pre, 0.0)
        squared = rounded(active * active)
        proj = jnp.dot(upstream, w_down.astype(jnp.float32).T)
        gate_part = rounded(jnp.sum((squared * proj).reshape(slots, N_HIDDEN, part_units), axis=2))
        gate_slot = jnp.sum(gate_part, axis=1)
        hidden_grad = rounded(weight * proj * 2.0 * active)
        grouped_up = up_f.reshape(LATENT, N_HIDDEN, part_units).transpose(1, 0, 2)
        latent_part = rounded(jnp.einsum('rgh,glh->rgl', hidden_grad.reshape(slots, N_HIDDEN, part_units), grouped_up))
        latent_slot = jnp.sum(latent_part, axis=1)
        scaled = rounded(weight * upstream)
        by_group_sq = squared.reshape(N_EXPERT, N_DP, CAP, HIDDEN_SIZE)
        by_group_sc = scaled.reshape(N_EXPERT, N_DP, CAP, LATENT)
        weight_part = rounded(jnp.einsum('edch,edcl->dhl', by_group_sq, by_group_sc))
        grad_total = grad_total.at[token].add(jnp.where(filled[:, None], latent_slot, 0.0))
        gate_total = gate_total.at[pick].add(jnp.where(filled, gate_slot, 0.0))
        return (grad_total, gate_total), jnp.sum(weight_part, axis=0)

    start = (jnp.zeros((TOKENS, LATENT), jnp.float32), jnp.zeros((TOKENS * TOP,), jnp.float32))
    (grad_total, gate_total), weight_grad = lax.scan(per_expert, start, (table, up_proj, down_proj))
    return grad_total, gate_total.reshape(TOKENS, TOP).astype(jnp.bfloat16), weight_grad
```

```python
import functools

import jax
import jax.numpy as jnp
from jax import lax
from jax.experimental import pallas as pl
from jax.experimental.pallas import tpu as pltpu
from jax.sharding import PartitionSpec as P


def rounded(value):
    return lax.optimization_barrier(value.astype(jnp.bfloat16)).astype(jnp.float32)


def body(
    inputs, out_grad, expert_ids, gate_weights, encode_weight, decode_weight, up_proj, down_proj
):
    owners = lax.axis_size("expert")
    local_experts = up_proj.shape[0]
    experts = local_experts * owners
    tokens_here = inputs.shape[0]
    picks = expert_ids.shape[1]
    capacity = max(2, tokens_here * picks * 7 // (experts * 6))
    slots = experts * capacity
    latent_in = jnp.dot(inputs, encode_weight, preferred_element_type=jnp.float32).astype(
        jnp.bfloat16
    )
    latent_out = lax.dot_general(
        out_grad, decode_weight, (((1,), (1,)), ((), ())), preferred_element_type=jnp.float32
    ).astype(jnp.bfloat16)
    flat_ids = expert_ids.reshape(-1)
    onehot = (flat_ids[:, None] == jnp.arange(experts, dtype=jnp.int32)[None, :]).astype(jnp.int32)
    earlier = jnp.cumsum(onehot, axis=0) - onehot
    slot_index = jnp.sum(earlier * onehot, axis=1)
    target = flat_ids * capacity + slot_index
    pick_count = flat_ids.shape[0]
    owner_pick = (
        jnp.full((slots,), -1, jnp.int32).at[target].set(jnp.arange(pick_count, dtype=jnp.int32))
    )
    filled = owner_pick >= 0
    safe_pick = jnp.maximum(owner_pick, 0)
    token_of = safe_pick // picks
    send_in = jnp.where(
        filled[:, None], jnp.take(latent_in, token_of, axis=0), jnp.zeros((), jnp.bfloat16)
    )
    send_out = jnp.where(
        filled[:, None], jnp.take(latent_out, token_of, axis=0), jnp.zeros((), jnp.bfloat16)
    )
    send_gate = jnp.where(
        filled, jnp.take(gate_weights.reshape(-1), safe_pick), jnp.zeros((), jnp.bfloat16)
    )
    recv_in, recv_out, recv_gate = (
        lax.all_to_all(send_in, "expert", split_axis=0, concat_axis=0, tiled=True),
        lax.all_to_all(send_out, "expert", split_axis=0, concat_axis=0, tiled=True),
        lax.all_to_all(send_gate, "expert", split_axis=0, concat_axis=0, tiled=True),
    )
    whole_in, whole_out = (
        lax.all_gather(recv_in, "hidden", axis=1, tiled=True),
        lax.all_gather(recv_out, "hidden", axis=1, tiled=True),
    )
    latent = whole_in.shape[1]
    encoded = whole_in.reshape(owners, local_experts, capacity, latent)
    upstream = whole_out.reshape(owners, local_experts, capacity, latent)
    weight = recv_gate.astype(jnp.float32).reshape(owners, local_experts, capacity, 1)
    pre = jnp.einsum("secl,elh->sech", encoded, up_proj, preferred_element_type=jnp.float32)
    active = jnp.maximum(pre, 0.0)
    squared = (active * active).astype(jnp.bfloat16)
    proj = jnp.einsum("secl,ehl->sech", upstream, down_proj, preferred_element_type=jnp.float32)
    gate_part = (
        jnp.sum(squared.astype(jnp.float32) * proj, axis=3).astype(jnp.bfloat16).reshape(slots)
    )
    hidden_grad = (weight * proj * 2.0 * active).astype(jnp.bfloat16)
    latent_part = jnp.einsum(
        "sech,elh->secl", hidden_grad, up_proj, preferred_element_type=jnp.float32
    ).reshape(slots, latent)
    scaled = (weight * upstream.astype(jnp.float32)).astype(jnp.bfloat16)
    weight_part = jnp.einsum("sech,secl->ehl", squared, scaled, preferred_element_type=jnp.float32)
    weight_grad = lax.psum_scatter(
        rounded(weight_part).astype(jnp.bfloat16), "dp", scatter_dimension=2, tiled=True
    ).astype(jnp.float32)
    slot_grad = lax.psum_scatter(
        rounded(latent_part).astype(jnp.bfloat16), "hidden", scatter_dimension=1, tiled=True
    ).astype(jnp.float32)
    back_grad, back_gate = (
        lax.all_to_all(
            slot_grad.astype(jnp.bfloat16), "expert", split_axis=0, concat_axis=0, tiled=True
        ).astype(slot_grad.dtype),
        lax.all_to_all(
            gate_part.astype(jnp.float32).astype(jnp.bfloat16),
            "expert",
            split_axis=0,
            concat_axis=0,
            tiled=True,
        ).astype(jnp.float32),
    )
    pick_grad = jnp.take(back_grad, target, axis=0)
    latent_grad = jnp.sum(pick_grad.reshape(tokens_here, picks, -1), axis=1)
    gate_local = jnp.take(back_gate, target).reshape(tokens_here, picks)
    gate_dots = lax.psum(gate_local, "hidden").astype(jnp.bfloat16)
    return (latent_grad, gate_dots, weight_grad)


LANES = 128
MESH = pl.DeviceIdType.MESH
(
    UP_S, DOWN_S, SIDE_S, DX_R, UY_S, DOWNY_S, SIDEY_S, DY_R, FX_S, FX_R, FY_S, FY_R,
    YX_S, YX_R, YY_S, YY_R, GX_S, GX_R, GY_S, GY_R, PS_S, PS_R, TS_S, TS_R,
) = range(24)
NT = (((1,), (1,)), ((), ()))
TN = (((0,), (0,)), ((), ()))


def dot(a, b, dims):
    return lax.dot_general(a, b, dims, preferred_element_type=jnp.float32)


def pad_rows(value, rows):
    extra = rows - value.shape[0]
    if extra == 0:
        return value
    return jnp.concatenate([value, jnp.zeros((extra, value.shape[1]), value.dtype)], axis=0)


def kernel(
    owners, chunks, steps,
    ids_hbm, gate_hbm, x_hbm, g_hbm, enc_hbm, dec_hbm, up_hbm, down_hbm,
    lat_ref, dots_ref, wg_ref,
    ids_ref, gate_ref, x_v, g_v, enc, dec, up, down, xg, yb, hgt, wt, gt, tr, lgo, ps, pr, ts, trb, sq_ref, sc_ref,
    sem, loc,
):
    me, h, d = lax.axis_index("expert"), lax.axis_index("hidden"), lax.axis_index("dp")
    local, units = up.shape[0], up.shape[1]
    half = enc.shape[1]
    picks, tokens = ids_ref.shape
    block = xg.shape[3]
    rows = owners * block
    piece = units // chunks
    other = {"hidden": 1 - h}
    across = {"dp": 1 - d}

    depth = enc.shape[0] // steps
    width = dec.shape[0] // steps
    copies = [pltpu.make_async_copy(x_hbm, x_v, loc.at[0])]
    for i in range(steps):
        part = pl.ds(i * depth, depth)
        copies.append(pltpu.make_async_copy(enc_hbm.at[part], enc.at[part], loc.at[1 + i]))
    copies.append(pltpu.make_async_copy(g_hbm, g_v, loc.at[1 + steps]))
    for i in range(steps):
        part = pl.ds(i * width, width)
        copies.append(pltpu.make_async_copy(dec_hbm.at[part], dec.at[part], loc.at[2 + steps + i]))
    copies.append(pltpu.make_async_copy(up_hbm, up, loc.at[2 + 2 * steps]))
    copies.append(pltpu.make_async_copy(down_hbm, down, loc.at[3 + 2 * steps]))
    small = [
        pltpu.make_async_copy(ids_hbm, ids_ref, loc.at[4 + 2 * steps]),
        pltpu.make_async_copy(gate_hbm, gate_ref, loc.at[5 + 2 * steps]),
    ]
    for copy in small + copies[: 2 + 2 * steps]:
        copy.start()

    live = pl.ds(0, tokens)
    spare = block - 16
    if tokens < block:
        xg[:, :, :, spare:block, :] = jnp.zeros((2, 2, owners, 16, half + LANES), jnp.bfloat16)
        yb[:, :, :, spare:block, :] = jnp.zeros((2, 2, owners, 16, half), jnp.bfloat16)

    barrier = pltpu.get_barrier_semaphore()
    for j in range(1, owners):
        pl.semaphore_signal(barrier, inc=1, device_id={"expert": lax.rem(me + j, owners)}, device_id_type=MESH)
    pl.semaphore_signal(barrier, inc=1, device_id=other, device_id_type=MESH)
    pl.semaphore_signal(barrier, inc=1, device_id=across, device_id_type=MESH)


    def remote(src, dst, s_kind, s_at, r_kind, r_at, device):
        return pltpu.make_async_remote_copy(
            src_ref=src, dst_ref=dst, send_sem=sem.at[s_kind, s_at], recv_sem=sem.at[r_kind, r_at],
            device_id=device, device_id_type=MESH,
        )

    side = lax.rem(me, 2)
    level, levels = me // 2, owners // 2
    aside = {"expert": me + 1 - 2 * side}
    above = {"expert": lax.rem(me + 2, owners)}
    below = {"expert": lax.rem(me + owners - 2, owners)}

    def x_same(at, s_kind, device):
        part = xg.at[0, h, at, live]
        return remote(part, part, s_kind, at, DX_R, at, device)

    def y_same(at, s_kind, device):
        part = yb.at[0, h, at, live]
        return remote(part, part, s_kind, at, DY_R, at, device)

    def x_pass(at):
        part = xg.at[0, h, at, live]
        return remote(part, part, FX_S, at, FX_R, at, other)

    def y_pass(at):
        part = yb.at[0, h, at, live]
        return remote(part, part, FY_S, at, FY_R, at, other)

    def x_across(at):
        return remote(xg.at[0, h, at, live], xg.at[1, h, at, live], YX_S, at, YX_R, at, across)

    def y_across(at):
        return remote(yb.at[0, h, at, live], yb.at[1, h, at, live], YY_S, at, YY_R, at, across)

    def x_far(at):
        part = xg.at[1, h, at, live]
        return remote(part, part, GX_S, at, GX_R, at, other)

    def y_far(at):
        part = yb.at[1, h, at, live]
        return remote(part, part, GY_S, at, GY_R, at, other)

    def x_near(at):
        x_pass(at).start()
        x_across(at).start()

    def y_near(at):
        y_pass(at).start()

        @pl.when(h == 1 - d)
        def _():
            y_across(at).start()

    def climb(at, move):
        @pl.when(level < levels - 1)
        def _():
            (x_same(at, UP_S, above) if move == "x" else y_same(at, UY_S, above)).start()

    def descend(at, move):
        @pl.when(level > 0)
        def _():
            (x_same(at, DOWN_S, below) if move == "x" else y_same(at, DOWNY_S, below)).start()

    def sideways(at, move):
        (x_same(at, SIDE_S, aside) if move == "x" else y_same(at, SIDEY_S, aside)).start()

    def arrived(at, move):
        (x_same(at, SIDE_S, aside) if move == "x" else y_same(at, SIDEY_S, aside)).wait_recv()

    small[0].wait()
    small[1].wait()
    expert_rows = lax.broadcasted_iota(jnp.int32, (LANES, tokens), 0)
    spread = jnp.zeros((LANES, tokens), jnp.float32)
    for k in range(picks):
        spread += jnp.where(
            ids_ref[k : k + 1, :] == expert_rows, gate_ref[k : k + 1, :].astype(jnp.float32), 0.0
        )
    tr[...] = jnp.zeros_like(tr)
    tr[:, 0:tokens] = spread
    own_gates = tr[...].T[0:block, :].astype(jnp.bfloat16)
    gt[...] = jnp.zeros_like(gt)

    copies[0].wait()
    total = jnp.zeros((tokens, half), jnp.float32)
    for i in range(steps):
        copies[1 + i].wait()
        total += jnp.dot(
            x_v[:, i * depth : (i + 1) * depth], enc[i * depth : (i + 1) * depth, :],
            preferred_element_type=jnp.float32,
        )
    xg[0, h, me, :, 0:half] = pad_rows(total, block).astype(jnp.bfloat16)
    xg[0, h, me, :, half : half + LANES] = own_gates
    copies[2 + 2 * steps].start()
    copies[3 + 2 * steps].start()
    pl.semaphore_wait(barrier, owners + 1)

    climb(me, "x")
    descend(me, "x")
    sideways(me, "x")
    x_near(me)

    copies[1 + steps].wait()
    for i in range(steps):
        copies[2 + steps + i].wait()
    for i in range(steps):
        got = dot(g_v[...], dec[i * width : (i + 1) * width, :], NT)
        yb[0, h, me, :, i * width : (i + 1) * width] = pad_rows(got, block).astype(jnp.bfloat16)

    climb(me, "y")
    descend(me, "y")
    sideways(me, "y")
    y_near(me)

    def relay(far, move):
        near = x_near if move == "x" else y_near

        @pl.when(level >= far)
        def _():
            at = me - 2 * far
            arrived(at, move)
            climb(at, move)
            sideways(at, move)
            near(at)

        @pl.when(level + far < levels)
        def _():
            at = me + 2 * far
            arrived(at, move)
            descend(at, move)
            sideways(at, move)
            near(at)

    def collect(far, move):
        near = x_near if move == "x" else y_near
        twin = me + 1 - 2 * side

        @pl.when(level >= far)
        def _():
            arrived(twin - 2 * far, move)
            near(twin - 2 * far)

        if far > 0:

            @pl.when(level + far < levels)
            def _():
                arrived(twin + 2 * far, move)
                near(twin + 2 * far)

    for far in range(1, levels):
        relay(far, "x")
        collect(far - 1, "x")
        relay(far, "y")
        collect(far - 1, "y")
    collect(levels - 1, "x")
    collect(levels - 1, "y")

    copies[2 + 2 * steps].wait()
    copies[3 + 2 * steps].wait()

    @pl.loop(0, owners)
    def _(s):
        remote(xg.at[0, 1 - h, s, live], xg.at[0, 1 - h, s, live], FX_S, s, FX_R, s, other).wait_recv()
        remote(yb.at[0, 1 - h, s, live], yb.at[0, 1 - h, s, live], FY_S, s, FY_R, s, other).wait_recv()

    def gates_of(side):
        return xg[side, h, :, :, half : half + LANES].reshape(rows, LANES).astype(jnp.float32)

    wt[...] = gates_of(0).T

    def pre_of(side, e, span):
        return dot(up[e, span, 0:half], xg[side, 0, :, :, 0:half].reshape(rows, half), NT) + dot(
            up[e, span, half : 2 * half], xg[side, 1, :, :, 0:half].reshape(rows, half), NT
        )

    @pl.loop(0, local * chunks)
    def _(step):
        e = step // chunks
        c = step % chunks
        span = pl.ds(pl.multiple_of(c * piece, piece), piece)
        active = jnp.maximum(pre_of(0, e, span), 0.0)
        squared = (active * active).astype(jnp.bfloat16)
        sq_ref[0, e, span, :] = squared
        proj = dot(down[e, span, 0:half], yb[0, 0].reshape(rows, half), NT) + dot(
            down[e, span, half : 2 * half], yb[0, 1].reshape(rows, half), NT
        )
        at = pl.ds(me * local + e, 1)
        gt[at, :] += jnp.sum(squared.astype(jnp.float32) * proj, axis=0, keepdims=True)
        grad = wt[at, :] * proj * 2.0 * active
        hgt[e, span, :] = grad.astype(jnp.bfloat16)

    @pl.loop(0, owners)
    def _(s):
        remote(xg.at[1, h, s, live], xg.at[1, h, s, live], YX_S, s, YX_R, s, across).wait_recv()
        x_far(s).start()

        @pl.when(h == d)
        def _():
            remote(yb.at[1, h, s, live], yb.at[1, h, s, live], YY_S, s, YY_R, s, across).wait_recv()
            y_far(s).start()

    tile = 2 * LANES if half % (2 * LANES) == 0 else LANES

    def latent_tile(which, t):
        column = pl.ds(pl.multiple_of(which * half + t * tile, tile), tile)
        out = dot(hgt[0], up[0, :, column], TN)
        for e in range(1, local):
            out += dot(hgt[e], up[e, :, column], TN)
        return out

    gate_cols = gt[...].T.astype(jnp.bfloat16)
    ps[:, :, half : half + LANES] = gate_cols.reshape(owners, block, LANES)

    @pl.loop(0, half // tile)
    def _(t):
        span = pl.ds(pl.multiple_of(t * tile, tile), tile)
        ps[:, :, span] = latent_tile(1 - h, t).astype(jnp.bfloat16).reshape(owners, block, tile)

    swap = remote(ps, pr, PS_S, 0, PS_R, 0, other)
    swap.start()

    @pl.loop(0, half // tile)
    def _(t):
        span = pl.ds(pl.multiple_of(t * tile, tile), tile)
        lgo[:, span] = latent_tile(h, t)

    swap.wait_recv()
    ts[:, :, 0:half] = (
        (lgo[...] + pr[:, :, 0:half].reshape(rows, half).astype(jnp.float32))
        .astype(jnp.bfloat16)
        .reshape(owners, block, half)
    )
    ts[:, :, half : half + LANES] = (
        (gate_cols.astype(jnp.float32) + pr[:, :, half : half + LANES].reshape(rows, LANES).astype(jnp.float32))
        .astype(jnp.bfloat16)
        .reshape(owners, block, LANES)
    )

    def give(at, s_at, r_at):
        return remote(ts.at[at, live], trb.at[r_at, live], TS_S, s_at, TS_R, r_at, {"expert": at})

    @pl.loop(1, owners)
    def _(j):
        peer = lax.rem(me + j, owners)
        give(peer, peer, me).start()

    trb[me] = ts[me]

    @pl.loop(0, owners)
    def _(s):
        remote(xg.at[1, 1 - h, s, live], xg.at[1, 1 - h, s, live], GX_S, s, GX_R, s, other).wait_recv()

        @pl.when(h == 1 - d)
        def _():
            remote(yb.at[1, 1 - h, s, live], yb.at[1, 1 - h, s, live], GY_S, s, GY_R, s, other).wait_recv()

    @pl.loop(0, local * chunks)
    def _(step):
        e = step // chunks
        c = step % chunks
        span = pl.ds(pl.multiple_of(c * piece, piece), piece)
        active = jnp.maximum(pre_of(1, e, span), 0.0)
        sq_ref[1, e, span, :] = (active * active).astype(jnp.bfloat16)

    lane = lax.broadcasted_iota(jnp.int32, (rows, LANES), 1)
    for part in range(2):
        gates = gates_of(part)
        mine = yb[part, d].reshape(rows, half).astype(jnp.float32)
        for e in range(local):
            column = jnp.sum(jnp.where(lane == me * local + e, gates, 0.0), axis=1, keepdims=True)
            sc_ref[part, e] = (column * mine).astype(jnp.bfloat16)

    @pl.loop(0, local * chunks)
    def _(step):
        e = step // chunks
        c = step % chunks
        span = pl.ds(pl.multiple_of(c * piece, piece), piece)
        wg_ref[e, span, :] = jnp.dot(
            sq_ref[0, e, span, :], sc_ref[0, e], preferred_element_type=jnp.float32
        ) + jnp.dot(sq_ref[1, e, span, :], sc_ref[1, e], preferred_element_type=jnp.float32)

    @pl.loop(1, owners)
    def _(j):
        s = lax.rem(me - j + owners, owners)
        give(s, s, s).wait_recv()

    final = trb[0].astype(jnp.float32)
    for s in range(1, owners):
        final += trb[s].astype(jnp.float32)
    lat_ref[...] = final[0:tokens, 0:half]
    tr[...] = jnp.zeros_like(tr)
    tr[0:block, :] = final[:, half : half + LANES]
    turned = tr[...].T[:, 0:tokens]
    picked = [
        jnp.sum(jnp.where(ids_ref[k : k + 1, :] == expert_rows, turned, 0.0), axis=0, keepdims=True)
        for k in range(picks)
    ]
    dots_ref[...] = jnp.concatenate(picked, axis=0).astype(jnp.bfloat16)
    swap.wait_send()

    @pl.loop(1, owners)
    def _(j):
        s = lax.rem(me + j, owners)
        give(s, s, s).wait_send()

    @pl.loop(0, owners)
    def _(s):
        x_pass(s).wait_send()
        y_pass(s).wait_send()
        x_across(s).wait_send()
        x_far(s).wait_send()

        @pl.when(h == 1 - d)
        def _():
            y_across(s).wait_send()

        @pl.when(h == d)
        def _():
            y_far(s).wait_send()

    @pl.loop(0, levels)
    def _(z):
        at = 2 * z + side
        x_same(at, SIDE_S, aside).wait_send()
        y_same(at, SIDEY_S, aside).wait_send()

        @pl.when((z <= level) & (level < levels - 1))
        def _():
            x_same(at, UP_S, above).wait_send()
            y_same(at, UY_S, above).wait_send()

        @pl.when((z >= level) & (level > 0))
        def _():
            x_same(at, DOWN_S, below).wait_send()
            y_same(at, DOWNY_S, below).wait_send()


def finish(lat_vmem, dots_vmem, wg_vmem, lat_ref, dots_ref, grad_ref, loc):
    moves = [
        pltpu.make_async_copy(wg_vmem, grad_ref, loc.at[0]),
        pltpu.make_async_copy(lat_vmem, lat_ref, loc.at[1]),
        pltpu.make_async_copy(dots_vmem, dots_ref, loc.at[2]),
    ]
    for move in moves:
        move.start()
    for move in moves:
        move.wait()


def dense_body(
    inputs, out_grad, expert_ids, gate_weights, encode_weight, decode_weight, up_proj, down_proj
):
    owners = lax.axis_size("expert")
    tokens, width = inputs.shape
    picks = expert_ids.shape[1]
    local, latent, units = up_proj.shape
    half = encode_weight.shape[1]
    block = -(-tokens // 16) * 16
    rows = owners * block
    chunks = 2 if units % 32 == 0 else 1
    steps = 4
    bf16, f32 = jnp.bfloat16, jnp.float32
    up_t = jnp.swapaxes(up_proj, 1, 2)
    vmem, hbm = pl.BlockSpec(memory_space=pltpu.VMEM), pl.BlockSpec(memory_space=pltpu.HBM)
    staged = [
        pltpu.with_memory_space_constraint(array, pltpu.HBM)
        for array in (expert_ids.T, gate_weights.T, inputs, out_grad, encode_weight, decode_weight, up_t, down_proj)
    ]
    parts = pl.pallas_call(
        functools.partial(kernel, owners, chunks, steps),
        out_shape=(
            pltpu.VMEM((tokens, half), f32),
            pltpu.VMEM((picks, tokens), bf16),
            pltpu.VMEM((local, units, half), f32),
        ),
        in_specs=[hbm] * 8,
        out_specs=(vmem, vmem, vmem),
        scratch_shapes=[
            pltpu.VMEM((picks, tokens), jnp.int32),
            pltpu.VMEM((picks, tokens), bf16),
            pltpu.VMEM((tokens, width), bf16),
            pltpu.VMEM((tokens, width), bf16),
            pltpu.VMEM((width, half), bf16),
            pltpu.VMEM((half, width), bf16),
            pltpu.VMEM((local, units, latent), bf16),
            pltpu.VMEM((local, units, latent), bf16),
            pltpu.VMEM((2, 2, owners, block, half + LANES), bf16),
            pltpu.VMEM((2, 2, owners, block, half), bf16),
            pltpu.VMEM((local, units, rows), bf16),
            pltpu.VMEM((LANES, rows), f32),
            pltpu.VMEM((LANES, rows), f32),
            pltpu.VMEM((LANES, LANES), f32),
            pltpu.VMEM((rows, half), f32),
            pltpu.VMEM((owners, block, half + LANES), bf16),
            pltpu.VMEM((owners, block, half + LANES), bf16),
            pltpu.VMEM((owners, block, half + LANES), bf16),
            pltpu.VMEM((owners, block, half + LANES), bf16),
            pltpu.VMEM((2, local, units, rows), bf16),
            pltpu.VMEM((2, local, rows, half), bf16),
            pltpu.SemaphoreType.DMA((24, owners)),
            pltpu.SemaphoreType.DMA((7 + 2 * steps,)),
        ],
        compiler_params=pltpu.CompilerParams(
            collective_id=0, has_side_effects=True, vmem_limit_bytes=48 * 2**20
        ),
    )(*staged)
    lat, dots, weight_grad = pl.pallas_call(
        finish,
        out_shape=(
            jax.ShapeDtypeStruct((tokens, half), f32),
            jax.ShapeDtypeStruct((picks, tokens), bf16),
            jax.ShapeDtypeStruct((local, units, half), f32),
        ),
        in_specs=[vmem] * 3,
        out_specs=(hbm, hbm, hbm),
        scratch_shapes=[pltpu.SemaphoreType.DMA((3,))],
        compiler_params=pltpu.CompilerParams(vmem_limit_bytes=2**20),
    )(*parts)
    return lat, dots.T, weight_grad


def pick_body(mesh):
    shape = mesh.shape
    fits = shape["hidden"] == 2 and shape["dp"] == 2 and shape["expert"] % 2 == 0
    return dense_body if fits else body


def solution(mesh):
    return jax.shard_map(
        pick_body(mesh),
        mesh=mesh,
        in_specs=(
            P(("expert", "dp"), None),
            P(("expert", "dp"), None),
            P(("expert", "dp"), None),
            P(("expert", "dp"), None),
            P(None, "hidden"),
            P("hidden", None),
            P("expert", None, "hidden"),
            P("expert", "hidden", None),
        ),
        out_specs=(
            P(("expert", "dp"), "hidden"),
            P(("expert", "dp"), None),
            P("expert", "hidden", "dp"),
        ),
        check_vma=False,
    )
```
